32 devices in a mesh: group: 4 (over y, x), member: 8 (over z, core).
Axes of the slice: x: 2, y: 2, z: 4, core: 2. Of those that a mesh axis runs over, the one named last changes fastest.
Arguments:
- factors: bfloat16 [4, 8192, 8192], P('group', 'member'), as said below
- owner: int32 [1], replicated, may hold values from 0 to 3
- grads: bfloat16 [8192, 512], P(None, 'group')
Outputs:
- new_factor: bfloat16 [8192, 8192], P('member', 'group')
The draws below stay inside these ranges and needn't reach their ends.
Inputs may be any that keep to these rules, and one draw needn't show every extreme that they name: `owner`: index of the group that owns the updated factor. `factors`: every group's factor is upper triangular with a positive diagonal.
All inputs are finite; a program needn't handle non-finite values.
Results may differ from the reference program's by a relative error of at most 0.0061.
Values may be sent and summed in bfloat16 or wider, within the bound.
A program may use at most 192 MiB of HBM per device.

```python
import math
import jax
import jax.numpy as jnp
from jax import lax

N = 8192
COLS = 512
N_GROUP = 4


def draw_factors(key, part):
    noise_key = jax.random.fold_in(key, 11)
    diag_key = jax.random.fold_in(key, 12)
    positions = jnp.arange(N)
    entries = jnp.clip(jax.random.normal(noise_key, (N_GROUP, N, N), jnp.float32), -4.0, 4.0)
    levels = jax.random.uniform(diag_key, (N_GROUP, 1, N), jnp.float32, math.log(0.7), math.log(1.4))
    diag_values = jnp.exp(levels) * (1.0 + 0.35 * positions.astype(jnp.float32) / N)
    above = positions[:, None] < positions[None, :]
    on_diag = positions[:, None] == positions[None, :]
    scaled = entries * (1.5 / math.sqrt(N))
    result = jnp.where(above[None], scaled, jnp.where(on_diag[None], diag_values, 0.0))
    return result.astype(jnp.bfloat16)


def draw_grads(key, part):
    base_key = jax.random.fold_in(key, 21)
    row_key = jax.random.fold_in(key, 22)
    col_key = jax.random.fold_in(key, 23)
    row_scale = jnp.exp(jax.random.uniform(row_key, (N, 1), jnp.float32, math.log(0.5), math.log(2.0)))
    base = jnp.clip(jax.random.normal(base_key, (N, COLS), jnp.float32), -4.0, 4.0)
    col_scale = jnp.exp(jax.random.uniform(col_key, (1, COLS), jnp.float32, math.log(0.3), math.log(3.0)))
    return (base * row_scale * col_scale).astype(jnp.bfloat16)


def setup_inputs(seed: int = 0) -> dict:
    streams_of = jax.random.split(jax.random.key(seed), 4)
    factors = draw_factors(jax.random.fold_in(streams_of[3], 71), 0)
    owner = jax.random.randint(streams_of[1], (1,), 0, N_GROUP).astype(jnp.int32)
    grads = draw_grads(jax.random.fold_in(streams_of[3], 71), 0)
    return dict(factors=factors, owner=owner, grads=grads)


step_size = 1.0


def reference(factors, owner, grads):
    factor = lax.dynamic_index_in_dim(factors, owner[0].astype(jnp.int32), 0, keepdims=False)
    projected = jnp.dot(factor, grads, preferred_element_type=jnp.float32).astype(jnp.bfloat16)
    precond = lax.dot_general(factor, projected, (((0,), (0,)), ((), ())), preferred_element_type=jnp.float32).astype(jnp.bfloat16)
    precond_wide = precond.astype(jnp.float32)
    gram = jnp.dot(precond, precond.T, preferred_element_type=jnp.float32)
    mean_square = jnp.sum(precond_wide * precond_wide) / (N * COLS)
    step_rate = step_size / (1.0 + mean_square)
    factor_wide = factor.astype(jnp.float32)
    combined = jnp.dot(jnp.triu(gram), factor_wide, precision=lax.Precision.HIGHEST)
    updated = (1.0 + step_rate) * factor_wide - (step_rate / COLS) * combined
    return updated.astype(jnp.bfloat16)
```

```python
import functools

import jax
import jax.numpy as jnp
from jax import lax
from jax.experimental import pallas as pl
from jax.experimental.pallas import tpu as pltpu
from jax.sharding import PartitionSpec as P

MESH = pl.DeviceIdType.MESH
step_size = 1.0


def serpentine(place):
    return (place // 2) * 2 + lax.rem(place + place // 2, 2)


def spread_kernel(root, groups, pieces, depth, f_ref, out_ref, stage, local_sem, send_sem, recv_sem):
    place = serpentine(lax.axis_index("group"))
    ahead = serpentine(lax.rem(place + 1, groups))
    behind = serpentine(lax.rem(place + groups - 1, groups))
    root_place = (root // 2) * 2 + (root + root // 2) % 2
    down = lax.rem(place - root_place + groups, groups)
    up = lax.rem(groups - down, groups)
    lanes = ((0, down, ahead), (1, up, behind))

    barrier = pltpu.get_barrier_semaphore()
    for neighbour in (ahead, behind):
        pl.semaphore_signal(barrier, inc=1, device_id={"group": neighbour}, device_id_type=MESH)
    pl.semaphore_wait(barrier, 2)

    def copy(source, side, piece, target):
        rows = pl.ds(pl.multiple_of((side * pieces + piece) * depth, depth), depth)
        return pltpu.make_async_remote_copy(
            src_ref=source.at[rows],
            dst_ref=out_ref.at[rows],
            send_sem=send_sem.at[side, piece],
            recv_sem=recv_sem.at[side, piece],
            device_id={"group": target},
            device_id_type=MESH,
        )

    @pl.when(down == 0)
    def _():
        @pl.loop(0, pieces)
        def _(piece):
            for side, _, target in lanes:
                copy(f_ref, side, piece, target).start()

        tall = stage.shape[0]

        @pl.loop(0, f_ref.shape[0] // tall)
        def _(block):
            rows = pl.ds(pl.multiple_of(block * tall, tall), tall)
            fetch = pltpu.make_async_copy(f_ref.at[rows], stage, local_sem.at[0])
            fetch.start()
            fetch.wait()
            store = pltpu.make_async_copy(stage, out_ref.at[rows], local_sem.at[1])
            store.start()
            store.wait()

        @pl.loop(0, pieces)
        def _(piece):
            for side, _, target in lanes:
                copy(f_ref, side, piece, target).wait_send()

    @pl.when(down > 0)
    def _():
        @pl.loop(0, pieces + groups - 2)
        def _(lap):
            for side, distance, target in lanes:
                piece = lap - distance + 1

                @pl.when((piece >= 0) & (piece < pieces))
                def _():
                    copy(out_ref, side, piece, target).wait_recv()

                    @pl.when(distance < groups - 1)
                    def _():
                        copy(out_ref, side, piece, target).start()

        @pl.loop(0, pieces)
        def _(piece):
            for side, distance, target in lanes:
                @pl.when(distance < groups - 1)
                def _():
                    copy(out_ref, side, piece, target).wait_send()


def spread(local_panel, owner, groups):
    rows, columns = local_panel.shape
    depth = 16
    pieces = rows // 2 // depth

    def branch(root, panel):
        return pl.pallas_call(
            functools.partial(spread_kernel, root, groups, pieces, depth),
            out_shape=jax.ShapeDtypeStruct((rows, columns), panel.dtype),
            in_specs=[pl.BlockSpec(memory_space=pl.ANY)],
            out_specs=pl.BlockSpec(memory_space=pl.ANY),
            scratch_shapes=[
                pltpu.VMEM((64, columns), panel.dtype),
                pltpu.SemaphoreType.DMA((2,)),
                pltpu.SemaphoreType.DMA((2, pieces)),
                pltpu.SemaphoreType.DMA((2, pieces)),
            ],
            compiler_params=pltpu.CompilerParams(
                collective_id=1 + root, has_side_effects=True, vmem_limit_bytes=4 * 2**20
            ),
            name=f"spread_{root}",
        )(panel)

    branches = [functools.partial(branch, root) for root in range(groups)]
    return lax.switch(owner, branches, local_panel)


def chain_kernel(
    members, pieces, term_ref, square_ref, tail_ref, total_ref,
    sibling, running, passed, given, other, slots,
    swap_send, swap_recv, run_send, run_recv, give_send, give_recv, square_send, square_recv,
):
    me = lax.axis_index("member")
    chip, core = me // 2, lax.rem(me, 2)
    chips = members // 2
    partner = chip * 2 + 1 - core
    below = lax.rem(me + members - 2, members)
    height, half = sibling.shape
    depth = height // pieces
    mine = pl.ds(pl.multiple_of(core * half, half), half)
    theirs = pl.ds(pl.multiple_of((1 - core) * half, half), half)

    barrier = pltpu.get_barrier_semaphore()
    for shift in range(1, members):
        pl.semaphore_signal(
            barrier, inc=1, device_id={"member": lax.rem(me + shift, members)}, device_id_type=MESH
        )
    pl.semaphore_wait(barrier, members - 1)

    def remote(source, target_ref, send, recv, target):
        return pltpu.make_async_remote_copy(
            src_ref=source, dst_ref=target_ref, send_sem=send, recv_sem=recv,
            device_id={"member": target}, device_id_type=MESH,
        )

    def rows_of(piece):
        return pl.ds(pl.multiple_of(piece * depth, depth), depth)

    def swap(piece):
        rows = rows_of(piece)
        return remote(
            term_ref.at[rows, theirs], sibling.at[rows], swap_send.at[piece], swap_recv.at[piece], partner
        )

    def run(piece):
        rows = rows_of(piece)
        return remote(passed.at[rows], running.at[rows], run_send.at[piece], run_recv.at[piece], below)

    def give(piece):
        rows = rows_of(piece)
        return remote(given.at[rows], other.at[rows], give_send.at[piece], give_recv.at[piece], partner)

    def square(shift, slot):
        return remote(
            square_ref, slots.at[slot], square_send.at[shift], square_recv.at[slot],
            lax.rem(me + shift, members),
        )

    @pl.loop(0, pieces)
    def _(piece):
        swap(piece).start()

    for shift in range(1, members):
        square(shift, me).start()

    @pl.when(chip == chips - 1)
    def _():
        running[...] = jnp.zeros_like(running)

    @pl.loop(0, pieces)
    def _(piece):
        rows = rows_of(piece)
        swap(piece).wait_recv()

        @pl.when(chip < chips - 1)
        def _():
            run(piece).wait_recv()

        late = running[rows, :].astype(jnp.float32)
        own = term_ref[rows, mine].astype(jnp.float32)
        beside = sibling[rows, :].astype(jnp.float32)

        @pl.when(chip > 0)
        def _():
            passed[rows, :] = (late + own + beside).astype(passed.dtype)
            run(piece).start()

        given[rows, :] = jnp.where(core == 1, late + own, late).astype(given.dtype)
        give(piece).start()
        tail_ref[rows, mine] = jnp.where(core == 0, late + beside, late).astype(tail_ref.dtype)

    @pl.loop(0, pieces)
    def _(piece):
        rows = rows_of(piece)
        give(piece).wait_recv()
        tail_ref[rows, theirs] = other[rows, :]
        swap(piece).wait_send()
        give(piece).wait_send()

        @pl.when(chip > 0)
        def _():
            run(piece).wait_send()

    total = square_ref[...]
    for shift in range(1, members):
        source = lax.rem(me + shift, members)
        square(shift, source).wait_recv()
        total = total + slots[source]
    total_ref[...] = total
    for shift in range(1, members):
        square(shift, me).wait_send()


def chain(term, squares, members, identifier):
    height, width = term.shape
    half = width // 2
    pieces = 8
    vmem = pl.BlockSpec(memory_space=pltpu.VMEM)
    buffer = pltpu.VMEM((height, half), term.dtype)
    sems = pltpu.SemaphoreType.DMA((pieces,))
    marks = pltpu.SemaphoreType.DMA((members,))
    return pl.pallas_call(
        functools.partial(chain_kernel, members, pieces),
        out_shape=(
            jax.ShapeDtypeStruct((height, width), term.dtype),
            jax.ShapeDtypeStruct(squares.shape, squares.dtype),
        ),
        in_specs=[vmem, vmem],
        out_specs=(vmem, vmem),
        scratch_shapes=[
            buffer, buffer, buffer, buffer, buffer,
            pltpu.VMEM((members, *squares.shape), squares.dtype),
            sems, sems, sems, sems, sems, sems, marks, marks,
        ],
        compiler_params=pltpu.CompilerParams(
            collective_id=identifier, has_side_effects=True, vmem_limit_bytes=32 * 2**20
        ),
        name="chain",
    )(term, squares)


def contract_rows(left_block, right_block):
    return lax.dot_general(
        left_block, right_block, (((0,), (0,)), ((), ())), preferred_element_type=jnp.float32
    )


def shards(groups, members, factors, owner, grads):
    factor_panel = spread(factors[0], owner[0], groups)
    projected = jnp.dot(factor_panel, grads, preferred_element_type=jnp.float32).astype(
        jnp.bfloat16
    )
    precond = lax.psum_scatter(
        contract_rows(factor_panel, projected), "member", scatter_dimension=0, tiled=True
    ).astype(jnp.bfloat16)
    factor_order = factor_panel.shape[1]
    total_columns = precond.shape[1] * groups
    block_width = factor_order // groups
    group_index = lax.axis_index("group")
    own_block = lax.dynamic_slice_in_dim(factor_panel, group_index * block_width, block_width, 1)
    left_rows = lax.all_gather(precond, "group", axis=1, tiled=True)
    left_wide = left_rows.astype(jnp.float32)
    squares = jnp.sum((left_wide * left_wide).reshape(-1, 8, left_wide.shape[1]), axis=0)
    terms = contract_rows(left_rows, own_block).astype(jnp.bfloat16)
    tail_total, square_sums = chain(terms, squares, members, groups + 1)
    diagonal_gram = jnp.triu(jnp.dot(left_rows, left_rows.T, preferred_element_type=jnp.float32))
    combined = jnp.dot(left_rows, tail_total, preferred_element_type=jnp.float32)
    combined = combined + jnp.dot(
        diagonal_gram.astype(jnp.bfloat16), own_block, preferred_element_type=jnp.float32
    )
    mean_square = jnp.sum(square_sums) / (factor_order * total_columns)
    step_rate = step_size / (1.0 + mean_square)
    updated = (1.0 + step_rate) * own_block.astype(
        jnp.float32
    ) - step_rate / total_columns * combined
    return updated.astype(jnp.bfloat16)


def solution(mesh):
    in_specs = (P("group", "member", None), P(), P(None, "group"))
    out_specs = P("member", "group")
    body = functools.partial(shards, mesh.shape["group"], mesh.shape["member"])
    return jax.shard_map(body, mesh=mesh, in_specs=in_specs, out_specs=out_specs, check_vma=False)
```

```python
import functools

import jax
import jax.numpy as jnp
from jax import lax
from jax.experimental import pallas as pl
from jax.experimental.pallas import tpu as pltpu
from jax.sharding import PartitionSpec as P

MESH = pl.DeviceIdType.MESH
step_size = 1.0


def serpentine(place):
    return (place // 2) * 2 + lax.rem(place + place // 2, 2)


def spread_kernel(
    root, groups, members, tall, f_ref, out_ref, aid_ref, stage, local_sem, zero_sem,
    send_sem, recv_sem, lend_send, lend_recv, aid_send, aid_recv, home_send, home_recv,
):
    rows, columns = f_ref.shape
    chips = members // 2
    wide = columns // chips
    blocks = rows // tall
    lent = blocks // 4
    me = lax.axis_index("member")
    chip = me // 2
    first, last = chip == 0, chip == chips - 1
    far = lax.rem(me + members - 2, members)
    near = lax.rem(me + 2, members)
    place = serpentine(lax.axis_index("group"))
    ahead = serpentine(lax.rem(place + 1, groups))
    behind = serpentine(lax.rem(place + groups - 1, groups))
    root_place = (root // 2) * 2 + (root + root // 2) % 2
    down = lax.rem(place - root_place + groups, groups)
    up = lax.rem(groups - down, groups)
    lanes = ((0, down, ahead), (1, up, behind))
    lent_side, full_side, short_side = lent // 2, blocks // 2, (blocks - lent) // 2
    count = jnp.where(first, short_side * chips, full_side * (chips - chip))

    barrier = pltpu.get_barrier_semaphore()
    for neighbour in (ahead, behind):
        pl.semaphore_signal(barrier, inc=1, device_id={"group": neighbour}, device_id_type=MESH)

    @pl.when(first)
    def _():
        pl.semaphore_signal(barrier, inc=1, device_id={"member": far}, device_id_type=MESH)

    @pl.when(last)
    def _():
        pl.semaphore_signal(barrier, inc=1, device_id={"member": near}, device_id_type=MESH)

    pl.semaphore_wait(barrier, 2 + jnp.where(first | last, 1, 0))

    def window(row, column):
        return (
            pl.ds(pl.multiple_of(row * tall, tall), tall),
            pl.ds(pl.multiple_of(column * wide, wide), wide),
        )

    def own(source, side, piece, target):
        row = jnp.where(
            first,
            side * short_side + piece % short_side,
            side * full_side + piece % full_side,
        )
        column = jnp.where(first, piece // short_side, chip + piece // full_side)
        spot = window(row, column)
        return pltpu.make_async_remote_copy(
            src_ref=source.at[spot], dst_ref=out_ref.at[spot],
            send_sem=send_sem.at[side, piece], recv_sem=recv_sem.at[side, piece],
            device_id={"group": target}, device_id_type=MESH,
        )

    def lent_spot(side, piece):
        return side * lent_side + piece % lent_side, piece // lent_side

    def lend(side, piece):
        row, column = lent_spot(side, piece)
        return pltpu.make_async_remote_copy(
            src_ref=f_ref.at[window(blocks - lent + row, column)],
            dst_ref=aid_ref.at[window(row, column)],
            send_sem=lend_send.at[side, piece], recv_sem=lend_recv.at[side, piece],
            device_id={"member": far}, device_id_type=MESH,
        )

    def aid(side, piece, target):
        spot = window(*lent_spot(side, piece))
        return pltpu.make_async_remote_copy(
            src_ref=aid_ref.at[spot], dst_ref=aid_ref.at[spot],
            send_sem=aid_send.at[side, piece], recv_sem=aid_recv.at[side, piece],
            device_id={"group": target}, device_id_type=MESH,
        )

    def home(side, piece):
        row, column = lent_spot(side, piece)
        return pltpu.make_async_remote_copy(
            src_ref=aid_ref.at[window(row, column)],
            dst_ref=out_ref.at[window(blocks - lent + row, column)],
            send_sem=home_send.at[side, piece], recv_sem=home_recv.at[side, piece],
            device_id={"member": near}, device_id_type=MESH,
        )

    lent_count = lent_side * chips

    @pl.when(down == 0)
    def _():
        @pl.when(first)
        def _():
            @pl.loop(0, lent_count)
            def _(piece):
                for side in (0, 1):
                    lend(side, piece).start()

        @pl.loop(0, count)
        def _(piece):
            for side, _, target in lanes:
                own(f_ref, side, piece, target).start()

        @pl.when(last)
        def _():
            @pl.loop(0, lent_count)
            def _(piece):
                for side, _, target in lanes:
                    lend(side, piece).wait_recv()
                    aid(side, piece, target).start()

        @pl.loop(0, chips)
        def _(column):
            lanes_of = pl.ds(pl.multiple_of(column * wide, wide), wide)
            fetch = pltpu.make_async_copy(f_ref.at[:, lanes_of], stage, local_sem.at[0])
            fetch.start()
            fetch.wait()
            store = pltpu.make_async_copy(stage, out_ref.at[:, lanes_of], local_sem.at[1])
            store.start()
            store.wait()

        @pl.loop(0, count)
        def _(piece):
            for side, _, target in lanes:
                own(f_ref, side, piece, target).wait_send()

        @pl.when(first)
        def _():
            @pl.loop(0, lent_count)
            def _(piece):
                for side in (0, 1):
                    lend(side, piece).wait_send()

        @pl.when(last)
        def _():
            @pl.loop(0, lent_count)
            def _(piece):
                for side, _, target in lanes:
                    aid(side, piece, target).wait_send()

    @pl.when(down > 0)
    def _():
        def blank(column):
            lanes_of = pl.ds(pl.multiple_of(column * wide, wide), wide)
            return pltpu.make_async_copy(stage, out_ref.at[:, lanes_of], zero_sem.at[column])

        @pl.when(chip > 0)
        def _():
            @pl.loop(0, blocks)
            def _(block):
                part = pl.ds(pl.multiple_of(block * tall, tall), tall)
                stage[part, :] = jnp.zeros((tall, wide), stage.dtype)

            @pl.loop(0, chip)
            def _(column):
                blank(column).start()

        @pl.loop(0, count + groups - 2)
        def _(lap):
            for side, distance, target in lanes:
                piece = lap - distance + 1

                @pl.when((piece >= 0) & (piece < count))
                def _():
                    own(out_ref, side, piece, target).wait_recv()

                    @pl.when(distance < groups - 1)
                    def _():
                        own(out_ref, side, piece, target).start()

        @pl.when(last)
        def _():
            @pl.loop(0, lent_count + groups - 2)
            def _(lap):
                for side, distance, target in lanes:
                    piece = lap - distance + 1

                    @pl.when((piece >= 0) & (piece < lent_count))
                    def _():
                        aid(side, piece, target).wait_recv()

                        @pl.when(distance < groups - 1)
                        def _():
                            aid(side, piece, target).start()

                        home(side, piece).start()

        @pl.when(first)
        def _():
            @pl.loop(0, lent_count)
            def _(piece):
                for side in (0, 1):
                    home(side, piece).wait_recv()

        @pl.loop(0, count)
        def _(piece):
            for side, distance, target in lanes:
                @pl.when(distance < groups - 1)
                def _():
                    own(out_ref, side, piece, target).wait_send()

        @pl.when(last)
        def _():
            @pl.loop(0, lent_count)
            def _(piece):
                for side, distance, target in lanes:
                    home(side, piece).wait_send()

                    @pl.when(distance < groups - 1)
                    def _():
                        aid(side, piece, target).wait_send()

        @pl.loop(0, chip)
        def _(column):
            blank(column).wait()


def spread(local_panel, owner, groups, members):
    rows, columns = local_panel.shape
    tall = 64
    chips = members // 2
    blocks = rows // tall
    lent = blocks // 4
    most = max((blocks - lent) // 2 * chips, blocks // 2 * (chips - 1))
    ring = pltpu.SemaphoreType.DMA((2, most))
    extra = pltpu.SemaphoreType.DMA((2, lent // 2 * chips))

    def branch(root, panel):
        return pl.pallas_call(
            functools.partial(spread_kernel, root, groups, members, tall),
            out_shape=(
                jax.ShapeDtypeStruct((rows, columns), panel.dtype),
                jax.ShapeDtypeStruct((lent * tall, columns), panel.dtype),
            ),
            in_specs=[pl.BlockSpec(memory_space=pl.ANY)],
            out_specs=(pl.BlockSpec(memory_space=pl.ANY), pl.BlockSpec(memory_space=pl.ANY)),
            scratch_shapes=[
                pltpu.VMEM((rows, columns // chips), panel.dtype),
                pltpu.SemaphoreType.DMA((2,)),
                pltpu.SemaphoreType.DMA((chips,)),
                ring, ring, extra, extra, extra, extra, extra, extra,
            ],
            compiler_params=pltpu.CompilerParams(
                collective_id=1 + root, has_side_effects=True, vmem_limit_bytes=12 * 2**20
            ),
            name=f"spread_{root}",
        )(panel)[0]

    branches = [functools.partial(branch, root) for root in range(groups)]
    return lax.switch(owner, branches, local_panel)


def chain_kernel(
    members, pieces, term_ref, square_ref, tail_ref, total_ref,
    sibling, running, passed, given, other, slots,
    swap_send, swap_recv, run_send, run_recv, give_send, give_recv, square_send, square_recv,
):
    me = lax.axis_index("member")
    chip, core = me // 2, lax.rem(me, 2)
    chips = members // 2
    partner = chip * 2 + 1 - core
    below = lax.rem(me + members - 2, members)
    height, half = sibling.shape
    depth = height // pieces
    mine = pl.ds(pl.multiple_of(core * half, half), half)
    theirs = pl.ds(pl.multiple_of((1 - core) * half, half), half)

    barrier = pltpu.get_barrier_semaphore()
    for shift in range(1, members):
        pl.semaphore_signal(
            barrier, inc=1, device_id={"member": lax.rem(me + shift, members)}, device_id_type=MESH
        )
    pl.semaphore_wait(barrier, members - 1)

    def remote(source, target_ref, send, recv, target):
        return pltpu.make_async_remote_copy(
            src_ref=source, dst_ref=target_ref, send_sem=send, recv_sem=recv,
            device_id={"member": target}, device_id_type=MESH,
        )

    def rows_of(piece):
        return pl.ds(pl.multiple_of(piece * depth, depth), depth)

    def swap(piece):
        rows = rows_of(piece)
        return remote(
            term_ref.at[rows, theirs], sibling.at[rows], swap_send.at[piece], swap_recv.at[piece], partner
        )

    def run(piece):
        rows = rows_of(piece)
        return remote(passed.at[rows], running.at[rows], run_send.at[piece], run_recv.at[piece], below)

    def give(piece):
        rows = rows_of(piece)
        return remote(given.at[rows], other.at[rows], give_send.at[piece], give_recv.at[piece], partner)

    def square(shift, slot):
        return remote(
            square_ref, slots.at[slot], square_send.at[shift], square_recv.at[slot],
            lax.rem(me + shift, members),
        )

    @pl.loop(0, pieces)
    def _(piece):
        swap(piece).start()

    for shift in range(1, members):
        square(shift, me).start()

    @pl.when(chip == chips - 1)
    def _():
        running[...] = jnp.zeros_like(running)

    @pl.loop(0, pieces)
    def _(piece):
        rows = rows_of(piece)
        swap(piece).wait_recv()

        @pl.when(chip < chips - 1)
        def _():
            run(piece).wait_recv()

        late = running[rows, :].astype(jnp.float32)
        own = term_ref[rows, mine].astype(jnp.float32)
        beside = sibling[rows, :].astype(jnp.float32)

        @pl.when(chip > 0)
        def _():
            passed[rows, :] = (late + own + beside).astype(passed.dtype)
            run(piece).start()

        given[rows, :] = jnp.where(core == 1, late + own, late).astype(given.dtype)
        give(piece).start()
        tail_ref[rows, mine] = jnp.where(core == 0, late + beside, late).astype(tail_ref.dtype)

    @pl.loop(0, pieces)
    def _(piece):
        rows = rows_of(piece)
        give(piece).wait_recv()
        tail_ref[rows, theirs] = other[rows, :]
        swap(piece).wait_send()
        give(piece).wait_send()

        @pl.when(chip > 0)
        def _():
            run(piece).wait_send()

    total = square_ref[...]
    for shift in range(1, members):
        source = lax.rem(me + shift, members)
        square(shift, source).wait_recv()
        total = total + slots[source]
    total_ref[...] = total
    for shift in range(1, members):
        square(shift, me).wait_send()


def chain(term, squares, members, identifier):
    height, width = term.shape
    half = width // 2
    pieces = 8
    vmem = pl.BlockSpec(memory_space=pltpu.VMEM)
    buffer = pltpu.VMEM((height, half), term.dtype)
    sems = pltpu.SemaphoreType.DMA((pieces,))
    marks = pltpu.SemaphoreType.DMA((members,))
    return pl.pallas_call(
        functools.partial(chain_kernel, members, pieces),
        out_shape=(
            jax.ShapeDtypeStruct((height, width), term.dtype),
            jax.ShapeDtypeStruct(squares.shape, squares.dtype),
        ),
        in_specs=[vmem, vmem],
        out_specs=(vmem, vmem),
        scratch_shapes=[
            buffer, buffer, buffer, buffer, buffer,
            pltpu.VMEM((members, *squares.shape), squares.dtype),
            sems, sems, sems, sems, sems, sems, marks, marks,
        ],
        compiler_params=pltpu.CompilerParams(
            collective_id=identifier, has_side_effects=True, vmem_limit_bytes=32 * 2**20
        ),
        name="chain",
    )(term, squares)


def contract_rows(left_block, right_block):
    return lax.dot_general(
        left_block, right_block, (((0,), (0,)), ((), ())), preferred_element_type=jnp.float32
    )


def shards(groups, members, factors, owner, grads):
    factor_panel = spread(factors[0], owner[0], groups, members)
    projected = jnp.dot(factor_panel, grads, preferred_element_type=jnp.float32).astype(
        jnp.bfloat16
    )
    partial_rows = contract_rows(projected, factor_panel)
    width = partial_rows.shape[0]
    split_rows = partial_rows.reshape(width, members, -1).transpose(1, 0, 2)
    precond = lax.psum_scatter(split_rows, "member", scatter_dimension=0, tiled=True)[0].astype(
        jnp.bfloat16
    )
    factor_order = factor_panel.shape[1]
    total_columns = width * groups
    block_width = factor_order // groups
    group_index = lax.axis_index("group")
    own_block = lax.dynamic_slice_in_dim(factor_panel, group_index * block_width, block_width, 1)
    left_rows = lax.all_gather(precond, "group", axis=0, tiled=True)
    left_wide = left_rows.astype(jnp.float32)
    squares = jnp.sum((left_wide * left_wide).reshape(-1, 8, left_wide.shape[1]), axis=0)
    terms = jnp.dot(left_rows, own_block, preferred_element_type=jnp.float32).astype(jnp.bfloat16)
    tail_total, square_sums = chain(terms, squares, members, groups + 1)
    diagonal_gram = jnp.triu(contract_rows(left_rows, left_rows))
    combined = contract_rows(left_rows, tail_total)
    combined = combined + jnp.dot(
        diagonal_gram.astype(jnp.bfloat16), own_block, preferred_element_type=jnp.float32
    )
    mean_square = jnp.sum(square_sums) / (factor_order * total_columns)
    step_rate = step_size / (1.0 + mean_square)
    updated = (1.0 + step_rate) * own_block.astype(
        jnp.float32
    ) - step_rate / total_columns * combined
    return updated.astype(jnp.bfloat16)


def solution(mesh):
    in_specs = (P("group", "member", None), P(), P(None, "group"))
    out_specs = P("member", "group")
    body = functools.partial(shards, mesh.shape["group"], mesh.shape["member"])
    return jax.shard_map(body, mesh=mesh, in_specs=in_specs, out_specs=out_specs, check_vma=False)
```
